32 devices in a mesh: ops: 4 (over x, core), sec: 8 (over z, y).
Axes of the slice: x: 2, y: 2, z: 4, core: 2. Of those that a mesh axis runs over, the one named last changes fastest.
Arguments:
- wavefunction: float32 [8, 640, 640], P('sec'), may hold values from -6 to 6
- left_ops: bfloat16 [8, 12, 640, 640], P('sec', 'ops'), may hold values from -0.3125 to 0.3125
- right_ops: bfloat16 [8, 12, 640, 640], P('sec', 'ops'), may hold values from -0.25 to 0.25
- charge_step: int32 [8, 12], P('sec', 'ops'), may hold values from -1 to 1
- sector_sizes: int32 [8], replicated, may hold values from 320 to 640
Outputs:
- cheb_prev: float32 [8, 640, 640], P('sec', 'ops')
- cheb_last: float32 [8, 640, 640], P('sec', 'ops')
The draws below stay inside these ranges and needn't reach their ends.
Inputs may be any that keep to these rules, and one draw needn't show every extreme that they name: Operator pair p of sector t reads sector t + charge_step[t, p].
All inputs are finite; a program needn't handle non-finite values.
Results may differ from the reference program's by a relative error of at most 0.0076.
Values may be sent and summed in bfloat16 or wider, within the bound.
A program may use at most 64 MiB of HBM per device.

```python
import jax
import jax.numpy as jnp
from jax import lax

W = 640
STEPS = 2
SECTORS = 8
PAIRS = 12


def place_ends(array, rng, low, largest):
    spot = [jax.random.randint(jax.random.fold_in(rng, axis), (), 0, length) for axis, length in enumerate(array.shape)]
    widest = array.shape.index(max(array.shape))
    beside = spot[:widest] + [(spot[widest] + 1) % array.shape[widest]] + spot[widest + 1:]
    return array.at[tuple(spot)].set(low).at[tuple(beside)].set(largest)


def strengthened(values, stream_key, source, target, blocks, factor):
    owner, partner = [(jnp.arange(values.shape[axis_at]) // (values.shape[axis_at] // blocks)).reshape([-1 if axis == axis_at else 1 for axis in range(values.ndim)]) for axis_at in (source, target)]
    chosen = jax.random.permutation(stream_key, blocks)[partner]
    strong = (owner == chosen) | (owner == (partner + blocks // 2) % blocks)
    return jnp.where(strong, factor * values, values)


def block_scale(stream_key, extent, pieces, smallest, high):
    level = 1.0
    for axis_at, parts in pieces:
        steps = jax.random.uniform(jax.random.fold_in(jax.random.fold_in(stream_key, 6), axis_at), (parts,), jnp.float32, smallest / len(pieces), high / len(pieces))
        level = level * jnp.repeat(jnp.exp(steps), extent[axis_at] // parts).reshape((-1,) + (1,) * (len(extent) - 1 - axis_at))
    return level


def gaussian(rng, shape, deviation, limit, pieces=(), kind=jnp.bfloat16):
    result = deviation * jax.random.normal(rng, shape, jnp.float32)
    if pieces:
        result = result * block_scale(rng, shape, pieces, -0.22, 0.18)
    return jnp.clip(result, -limit, limit).astype(kind)


def bell_draw_with(stream_key, shape, deviation, bound, pieces, heavy, kind=jnp.bfloat16):
    entries = deviation * jax.random.normal(stream_key, shape, jnp.float32)
    if pieces:
        entries = entries * block_scale(stream_key, shape, pieces, -0.22, 0.18)
    return jnp.clip(strengthened(entries, jax.random.fold_in(stream_key, 3), *heavy), -bound, bound).astype(kind)


def setup_inputs(seed: int = 0) -> dict:
    streams_of = jax.random.split(jax.random.key(seed), 6)
    return {
        "wavefunction": gaussian(streams_of[0], (SECTORS, W, W), 1.0, 6.0, ((0, 8),), jnp.float32),
        "left_ops": bell_draw_with(streams_of[1], (SECTORS, PAIRS, W, W), W ** -0.5, 0.3125, ((0, 8), (1, 4)), (1, 2, 4, 2.0)),
        "right_ops": gaussian(streams_of[2], (SECTORS, PAIRS, W, W), W ** -0.5, 0.25, ((0, 8), (1, 4))),
        "charge_step": place_ends(jax.random.randint(streams_of[3], (SECTORS, PAIRS), -1, 2), jax.random.fold_in(streams_of[3], 1), -1, 1).astype(jnp.int32),
        "sector_sizes": place_ends(jax.random.randint(streams_of[4], (SECTORS,), W // 2, W + 1), jax.random.fold_in(streams_of[4], 1), W // 2, W).astype(jnp.int32),
    }


def live_masks(sector_sizes):
    live_rows = (jnp.arange(W, dtype=jnp.int32)[None, :] < sector_sizes[:, None]).astype(jnp.float32)
    return live_rows[:, :, None] * live_rows[:, None, :]


def hamiltonian(vector, left_ops, right_ops, charge_step, live_mask):
    rounded = vector.astype(jnp.bfloat16).astype(jnp.float32)
    padded = jnp.pad(rounded, ((1, 1), (0, 0), (0, 0)))
    norm_scale = 1.0 / (PAIRS ** 0.5)

    def sector(sector_index):
        nearby = lax.dynamic_slice_in_dim(padded, sector_index, 3, 0)
        onehot = (charge_step[sector_index][:, None] + 1 == jnp.arange(3, dtype=jnp.int32)[None, :]).astype(jnp.float32)
        inputs = jnp.einsum("pc,cab->pab", onehot, nearby, precision=lax.Precision.HIGHEST)
        left_block = left_ops[sector_index].astype(jnp.float32)
        left_half = jnp.einsum("pab,pbc->pac", left_block, inputs, precision=lax.Precision.HIGHEST)
        left_half = left_half.astype(jnp.bfloat16).astype(jnp.float32)
        right_block = right_ops[sector_index].astype(jnp.float32)
        summed = jnp.einsum("pac,pdc->ad", left_half, right_block, precision=lax.Precision.HIGHEST)
        return summed * norm_scale * live_mask[sector_index]

    return lax.map(sector, jnp.arange(SECTORS, dtype=jnp.int32))


def reference(wavefunction, left_ops, right_ops, charge_step, sector_sizes):
    live_mask = live_masks(sector_sizes)
    start_field = wavefunction * live_mask
    previous = start_field
    current = hamiltonian(start_field, left_ops, right_ops, charge_step, live_mask)
    for iteration in range(1, STEPS):
        updated = 2.0 * hamiltonian(current, left_ops, right_ops, charge_step, live_mask) - previous
        previous, current = current, updated
    return previous, current
```

```python
import functools
import math

import jax
import jax.numpy as jnp
from jax import lax
from jax.experimental import pallas as pl
from jax.experimental.pallas import tpu as pltpu
from jax.sharding import PartitionSpec as P

STEPS = 2
CORES = 2
PIECES = 2
ROW_TILE = 16
MESH_ID = pl.DeviceIdType.MESH


def padded(shard, sides, width):
    for axis, dim in sides:
        peers, length = (lax.axis_size(axis), shard.shape[dim])
        up = [(i, (i + 1) % peers) for i in range(peers - 1)]
        down = [(j, i) for i, j in up]
        last = lax.slice_in_dim(shard, length - width, length, axis=dim)
        initial = lax.slice_in_dim(shard, 0, width, axis=dim)
        before = lax.ppermute(last, axis, up)
        after = lax.ppermute(initial, axis, down)
        shard = jnp.concatenate([before, shard, after], axis=dim)
    return shard


def by_collectives(wavefunction, left_ops, right_ops, charge_step, sector_sizes):
    ops_count = lax.axis_size("ops")
    width_all = wavefunction.shape[1]
    share_rows = width_all // ops_count
    first_row = lax.axis_index("ops") * share_rows
    own_size = lax.dynamic_index_in_dim(sector_sizes, lax.axis_index("sec"), 0, keepdims=False)
    positions = jnp.arange(width_all, dtype=jnp.int32)
    live_cols = (positions < own_size).astype(jnp.float32)
    row_live = lax.dynamic_slice_in_dim(live_cols, first_row, share_rows, 0)
    full_mask = live_cols[:, None] * live_cols[None, :]
    row_mask = row_live[:, None] * live_cols[None, :]
    norm_scale = 1.0 / math.sqrt(left_ops.shape[1] * ops_count)
    onehot = (charge_step[0][:, None] + 1 == jnp.arange(3, dtype=jnp.int32)[None, :]).astype(
        jnp.bfloat16
    )
    start_field = wavefunction[0] * full_mask
    start_rows = lax.dynamic_slice_in_dim(start_field, first_row, share_rows, 0)
    previous = start_rows
    current = start_rows
    source_full = start_field.astype(jnp.bfloat16)
    for iteration in range(STEPS):
        nearby = padded(source_full[None], (("sec", 0),), 1)
        inputs = jnp.einsum(
            "pc,cab->pab", onehot, nearby, preferred_element_type=jnp.float32
        ).astype(jnp.bfloat16)
        left_half = jnp.einsum(
            "pab,pbc->pac", left_ops[0], inputs, preferred_element_type=jnp.float32
        ).astype(jnp.bfloat16)
        summed = lax.psum_scatter(
            jnp.einsum("pac,pdc->ad", left_half, right_ops[0], preferred_element_type=jnp.float32),
            "ops",
            scatter_dimension=0,
            tiled=True,
        )
        applied = summed * norm_scale * row_mask
        updated = applied if iteration == 0 else 2.0 * applied - previous
        previous = start_rows if iteration == 0 else current
        current = updated
        if iteration + 1 < STEPS:
            source_full = lax.all_gather(updated.astype(jnp.bfloat16), "ops", axis=0, tiled=True)
    return (previous[None], current[None])


def kernel(
    ops_count, sectors,
    v_hbm, l_hbm, r_hbm, charge_ref, size_ref, prev_ref, last_ref,
    v_buf, l_buf, r_buf, xa0, xb0, xa1, xb1, y_buf,
    acc_far, acc_near, to_mate, from_mate, to_chip, from_chip,
    local_sem, send_sem, recv_sem,
):
    pairs, width = l_hbm.shape[1], l_hbm.shape[2]
    share = width // ops_count
    half = CORES * share
    piece = share // PIECES
    scale = 1.0 / math.sqrt(pairs * ops_count)

    o = lax.axis_index("ops")
    t = lax.axis_index("sec")
    core = lax.rem(o, CORES)
    chip = o // CORES
    mate = o + 1 - 2 * core
    across = lax.rem(o + CORES, ops_count)
    parity = lax.rem(t, 2)
    direct_to = t + 1 - 2 * parity
    relay_to = t + 2 - 4 * parity
    relay_from = t - 2 + 4 * parity
    has_target = jnp.logical_and(relay_to >= 0, relay_to < sectors)
    has_source = jnp.logical_and(relay_from >= 0, relay_from < sectors)

    v_copy = pltpu.make_async_copy(v_hbm.at[0], v_buf, local_sem.at[0])
    v_copy.start()
    loads = []
    for p in range(pairs):
        loads.append(pltpu.make_async_copy(r_hbm.at[0, p], r_buf.at[p], local_sem.at[1 + p]))
    for p in range(pairs):
        loads.append(pltpu.make_async_copy(
            l_hbm.at[0, p], l_buf.at[:, pl.ds(p * width, width)], local_sem.at[1 + pairs + p]))
    for load in loads:
        load.start()

    barrier = pltpu.get_barrier_semaphore()
    pl.semaphore_signal(barrier, inc=1, device_id={"ops": mate}, device_id_type=MESH_ID)
    pl.semaphore_signal(barrier, inc=1, device_id={"ops": across}, device_id_type=MESH_ID)
    pl.semaphore_signal(barrier, inc=1, device_id={"sec": direct_to}, device_id_type=MESH_ID)

    @pl.when(has_target)
    def _():
        pl.semaphore_signal(barrier, inc=1, device_id={"sec": relay_to}, device_id_type=MESH_ID)

    @pl.when(has_source)
    def _():
        pl.semaphore_signal(barrier, inc=1, device_id={"sec": relay_from}, device_id_type=MESH_ID)

    size = size_ref[t]
    cols_live = lax.broadcasted_iota(jnp.int32, (1, width), 1) < size

    def masked(value, first):
        rows = first + lax.broadcasted_iota(jnp.int32, (value.shape[0], 1), 0)
        return jnp.where(jnp.logical_and(rows < size, cols_live), value, 0.0)

    def aligned(start, length):
        return pl.ds(pl.multiple_of(start, ROW_TILE), length)

    fields = ((xa0, xb0), (xa1, xb1))
    chips = (chip, 1 - chip)

    @pl.when(jnp.logical_not(has_source))
    def _():
        for field in fields:
            for x in field:
                x[2] = jnp.zeros(x.shape[1:], x.dtype)

    counter = [0]
    started = []

    def remote(src, dst, target):
        i = counter[0]
        counter[0] += 1
        return pltpu.make_async_remote_copy(
            src_ref=src, dst_ref=dst, send_sem=send_sem.at[i], recv_sem=recv_sem.at[i],
            device_id=target, device_id_type=MESH_ID)

    def go(copy):
        copy.start()
        started.append((copy, False))

    mine = [aligned(core * share + h * piece, piece) for h in range(PIECES)]
    grid = [(g, h) for g in range(2) for h in range(PIECES)]
    plans = []
    for field in fields:
        plan = {"direct": {}, "relay": {}, "mate0": {}, "mate1": {}, "mate2": {}, "across": {}}
        for g, h in grid:
            x, rows = field[g], mine[h]
            plan["direct"][g, h] = remote(x.at[1, rows], x.at[0, rows], {"sec": direct_to})
            plan["relay"][g, h] = remote(x.at[0, rows], x.at[2, rows], {"sec": relay_to})
            for slot in range(3):
                plan[f"mate{slot}"][g, h] = remote(
                    x.at[slot, rows], x.at[slot, rows], {"ops": mate})
        for h in range(PIECES):
            plan["across"][h] = remote(
                field[0].at[1, mine[h]], field[1].at[1, mine[h]], {"ops": across})
        plans.append(plan)

    def direct_in(plan, g, h):
        plan["direct"][g, h].wait_recv()

        @pl.when(has_target)
        def _():
            plan["relay"][g, h].start()

        started.append((plan["relay"][g, h], True))
        go(plan["mate0"][g, h])

    def relay_in(plan, g, h):
        @pl.when(has_source)
        def _():
            plan["relay"][g, h].wait_recv()
            plan["mate2"][g, h].start()

    def mates_in(step, plan, g):
        for h in range(PIECES):
            if step:
                plan["mate1"][g, h].wait_recv()
            plan["mate0"][g, h].wait_recv()

        @pl.when(has_source)
        def _():
            for h in range(PIECES):
                plan["mate2"][g, h].wait_recv()

    picks = [1 - (1 - 2 * parity) * charge_ref[0, p] for p in range(pairs)]

    def right_products(step, g):
        x = fields[step][g]
        for p in range(pairs):
            y_buf[aligned(p * width + chips[g] * half, half), :] = lax.dot_general(
                x[picks[p]], r_buf[p], (((1,), (1,)), ((), ())),
                preferred_element_type=jnp.float32).astype(jnp.bfloat16)

    def left_products(g):
        return jnp.dot(l_buf[aligned(chips[g] * half, half), :], y_buf[...],
                       preferred_element_type=jnp.float32)

    v_copy.wait()
    for g in range(2):
        first = chips[g] * half
        xs = v_buf[aligned(first, half), :]
        fields[0][g][1] = masked(xs, first).astype(jnp.bfloat16)
    pl.semaphore_wait(barrier, 3 + has_target.astype(jnp.int32) + has_source.astype(jnp.int32))

    for g, h in grid:
        go(plans[0]["direct"][g, h])

    for step in range(STEPS):
        plan = plans[step]
        for i, (g, h) in enumerate(grid):
            if step and g == 0:
                plan["across"][h].wait_recv()
                go(plan["direct"][1, h])
                go(plan["mate1"][1, h])
            direct_in(plan, g, h)
            if i and grid[i - 1][0] == 0:
                relay_in(plan, *grid[i - 1])
        if not step:
            for load in loads[:pairs]:
                load.wait()
        mates_in(step, plan, 0)
        right_products(step, 0)
        for h in range(PIECES):
            relay_in(plan, 1, h)
        mates_in(step, plan, 1)
        right_products(step, 1)
        if not step:
            for load in loads[pairs:]:
                load.wait()

        theirs = aligned((1 - core) * share, share)
        hand = [remote(to_mate.at[step, k], from_mate.at[step, k], {"ops": mate}) for k in range(2)]
        acc_far[...] = left_products(1)
        to_mate[step, 0] = acc_far[theirs, :].astype(jnp.bfloat16)
        go(hand[0])
        acc_near[...] = left_products(0)
        to_mate[step, 1] = acc_near[theirs, :].astype(jnp.bfloat16)
        go(hand[1])
        hand[0].wait_recv()
        ship = []
        for h in range(PIECES):
            part = pl.ds(h * piece, piece)
            to_chip[step, part, :] = (
                acc_far[mine[h], :] + from_mate[step, 0, part, :].astype(jnp.float32)
            ).astype(jnp.bfloat16)
            ship.append(remote(to_chip.at[step, part], from_chip.at[step, part], {"ops": across}))
            go(ship[h])
        hand[1].wait_recv()
        for h in range(PIECES):
            part = pl.ds(h * piece, piece)
            first = o * share + h * piece
            ship[h].wait_recv()
            summed = (
                acc_near[mine[h], :]
                + from_mate[step, 1, part, :].astype(jnp.float32)
                + from_chip[step, part, :].astype(jnp.float32)
            )
            applied = masked(summed * scale, first)
            if step == 0:
                prev_ref[0, part, :] = applied
                xa1[1, mine[h], :] = applied.astype(jnp.bfloat16)
                following = plans[1]
                go(following["direct"][0, h])
                go(following["across"][h])
                go(following["mate1"][0, h])
            else:
                start_rows = masked(v_buf[aligned(first, piece), :], first)
                last_ref[0, part, :] = 2.0 * applied - start_rows

    for copy, relayed in started:
        if not relayed:
            copy.wait_send()

    @pl.when(has_target)
    def _():
        for copy, relayed in started:
            if relayed:
                copy.wait_send()

    @pl.when(has_source)
    def _():
        for plan in plans:
            for g, h in grid:
                plan["mate2"][g, h].wait_send()


def by_kernel(wavefunction, left_ops, right_ops, charge_step, sector_sizes):
    ops_count, sectors = lax.axis_size("ops"), lax.axis_size("sec")
    pairs, width = left_ops.shape[1], left_ops.shape[2]
    share = width // ops_count
    half = CORES * share
    anywhere = pl.BlockSpec(memory_space=pl.ANY)
    scalars = pl.BlockSpec(memory_space=pltpu.SMEM)
    vmem = pl.BlockSpec(memory_space=pltpu.VMEM)
    bf16, f32 = jnp.bfloat16, jnp.float32
    field = pltpu.VMEM((3, half, width), bf16)
    copies = STEPS * (2 * PIECES * 5 + PIECES + 2 + PIECES)
    out = jax.ShapeDtypeStruct((1, share, width), f32)
    return pl.pallas_call(
        functools.partial(kernel, ops_count, sectors),
        out_shape=(out, out),
        in_specs=[anywhere, anywhere, anywhere, scalars, scalars],
        out_specs=(vmem, vmem),
        scratch_shapes=[
            pltpu.VMEM((width, width), f32),
            pltpu.VMEM((width, pairs * width), bf16),
            pltpu.VMEM((pairs, width, width), bf16),
            field, field, field, field,
            pltpu.VMEM((pairs * width, width), bf16),
            pltpu.VMEM((half, width), f32),
            pltpu.VMEM((half, width), f32),
            pltpu.VMEM((STEPS, 2, share, width), bf16),
            pltpu.VMEM((STEPS, 2, share, width), bf16),
            pltpu.VMEM((STEPS, share, width), bf16),
            pltpu.VMEM((STEPS, share, width), bf16),
            pltpu.SemaphoreType.DMA((1 + 2 * pairs,)),
            pltpu.SemaphoreType.DMA((copies,)),
            pltpu.SemaphoreType.DMA((copies,)),
        ],
        compiler_params=pltpu.CompilerParams(
            collective_id=0, has_side_effects=True, vmem_limit_bytes=48 * 1024 * 1024),
    )(wavefunction, left_ops, right_ops, charge_step, sector_sizes)


def on_device(wavefunction, left_ops, right_ops, charge_step, sector_sizes):
    ops_count, sectors = lax.axis_size("ops"), lax.axis_size("sec")
    share = wavefunction.shape[1] // ops_count
    paired = ops_count == 2 * CORES and sectors % 2 == 0
    tiled = share % (PIECES * ROW_TILE) == 0
    body = by_kernel if paired and tiled else by_collectives
    return body(wavefunction, left_ops, right_ops, charge_step, sector_sizes)


def solution(mesh):
    in_specs = (
        P("sec", None, None),
        P("sec", "ops", None, None),
        P("sec", "ops", None, None),
        P("sec", "ops"),
        P(),
    )
    out_specs = (P("sec", "ops", None), P("sec", "ops", None))
    return jax.shard_map(
        on_device, mesh=mesh, in_specs=in_specs, out_specs=out_specs, check_vma=False
    )
```

```python
import functools
import math

import jax
import jax.numpy as jnp
from jax import lax
from jax.experimental import pallas as pl
from jax.experimental.pallas import tpu as pltpu
from jax.sharding import PartitionSpec as P

STEPS = 2
CORES = 2
PIECES = 5
STRAIGHT = 2
ROW_TILE = 16
MESH_ID = pl.DeviceIdType.MESH


def padded(shard, sides, width):
    for axis, dim in sides:
        peers, length = (lax.axis_size(axis), shard.shape[dim])
        up = [(i, (i + 1) % peers) for i in range(peers - 1)]
        down = [(j, i) for i, j in up]
        last = lax.slice_in_dim(shard, length - width, length, axis=dim)
        initial = lax.slice_in_dim(shard, 0, width, axis=dim)
        before = lax.ppermute(last, axis, up)
        after = lax.ppermute(initial, axis, down)
        shard = jnp.concatenate([before, shard, after], axis=dim)
    return shard


def by_collectives(wavefunction, left_ops, right_ops, charge_step, sector_sizes):
    ops_count = lax.axis_size("ops")
    width_all = wavefunction.shape[1]
    share_rows = width_all // ops_count
    first_row = lax.axis_index("ops") * share_rows
    own_size = lax.dynamic_index_in_dim(sector_sizes, lax.axis_index("sec"), 0, keepdims=False)
    positions = jnp.arange(width_all, dtype=jnp.int32)
    live_cols = (positions < own_size).astype(jnp.float32)
    row_live = lax.dynamic_slice_in_dim(live_cols, first_row, share_rows, 0)
    full_mask = live_cols[:, None] * live_cols[None, :]
    row_mask = row_live[:, None] * live_cols[None, :]
    norm_scale = 1.0 / math.sqrt(left_ops.shape[1] * ops_count)
    onehot = (charge_step[0][:, None] + 1 == jnp.arange(3, dtype=jnp.int32)[None, :]).astype(
        jnp.bfloat16
    )
    start_field = wavefunction[0] * full_mask
    start_rows = lax.dynamic_slice_in_dim(start_field, first_row, share_rows, 0)
    previous = start_rows
    current = start_rows
    source_full = start_field.astype(jnp.bfloat16)
    for iteration in range(STEPS):
        nearby = padded(source_full[None], (("sec", 0),), 1)
        inputs = jnp.einsum(
            "pc,cab->pab", onehot, nearby, preferred_element_type=jnp.float32
        ).astype(jnp.bfloat16)
        left_half = jnp.einsum(
            "pab,pbc->pac", left_ops[0], inputs, preferred_element_type=jnp.float32
        ).astype(jnp.bfloat16)
        summed = lax.psum_scatter(
            jnp.einsum("pac,pdc->ad", left_half, right_ops[0], preferred_element_type=jnp.float32),
            "ops",
            scatter_dimension=0,
            tiled=True,
        )
        applied = summed * norm_scale * row_mask
        updated = applied if iteration == 0 else 2.0 * applied - previous
        previous = start_rows if iteration == 0 else current
        current = updated
        if iteration + 1 < STEPS:
            source_full = lax.all_gather(updated.astype(jnp.bfloat16), "ops", axis=0, tiled=True)
    return (previous[None], current[None])


def kernel(
    ops_count, sectors,
    v_hbm, l_hbm, r_hbm, charge_hbm, size_hbm, prev_ref, last_ref,
    charge_ref, size_ref, v_buf, l_buf, r_buf, xa0, xm0, xb0, xn0, xa1, xm1, xb1, xn1, y_buf,
    acc_far, acc_near, to_mate, from_mate, to_chip, from_chip, to_twin, from_twin,
    local_sem, send_sem, recv_sem,
):
    pairs, width = l_hbm.shape[1], l_hbm.shape[2]
    share = width // ops_count
    half = CORES * share
    piece = share // PIECES
    scale = 1.0 / math.sqrt(pairs * ops_count)

    o = lax.axis_index("ops")
    t = lax.axis_index("sec")
    core = lax.rem(o, CORES)
    chip = o // CORES
    mate = o + 1 - 2 * core
    across = lax.rem(o + CORES, ops_count)
    parity = lax.rem(t, 2)
    direct_to = t + 1 - 2 * parity
    relay_to = t + 2 - 4 * parity
    relay_from = t - 2 + 4 * parity
    has_target = jnp.logical_and(relay_to >= 0, relay_to < sectors)
    has_source = jnp.logical_and(relay_from >= 0, relay_from < sectors)

    v_copy = pltpu.make_async_copy(v_hbm.at[0], v_buf, local_sem.at[0])
    smalls = [pltpu.make_async_copy(size_hbm, size_ref, local_sem.at[1 + 2 * pairs]),
              pltpu.make_async_copy(charge_hbm, charge_ref, local_sem.at[2 + 2 * pairs])]
    v_copy.start()
    for small in smalls:
        small.start()
    loads = []
    for p in range(pairs):
        loads.append(pltpu.make_async_copy(r_hbm.at[0, p], r_buf.at[p], local_sem.at[1 + p]))
    for p in range(pairs):
        loads.append(pltpu.make_async_copy(
            l_hbm.at[0, p], l_buf.at[:, pl.ds(p * width, width)], local_sem.at[1 + pairs + p]))

    barrier = pltpu.get_barrier_semaphore()
    pl.semaphore_signal(barrier, inc=1, device_id={"ops": mate}, device_id_type=MESH_ID)
    pl.semaphore_signal(barrier, inc=1, device_id={"ops": across}, device_id_type=MESH_ID)
    pl.semaphore_signal(barrier, inc=1, device_id={"sec": direct_to}, device_id_type=MESH_ID)

    @pl.when(has_target)
    def _():
        pl.semaphore_signal(barrier, inc=1, device_id={"sec": relay_to}, device_id_type=MESH_ID)

    @pl.when(has_source)
    def _():
        pl.semaphore_signal(barrier, inc=1, device_id={"sec": relay_from}, device_id_type=MESH_ID)

    for small in smalls:
        small.wait()
    size = size_ref[t]
    cols_live = lax.broadcasted_iota(jnp.int32, (1, width), 1) < size

    def masked(value, first):
        rows = first + lax.broadcasted_iota(jnp.int32, (value.shape[0], 1), 0)
        return jnp.where(jnp.logical_and(rows < size, cols_live), value, 0.0)

    def aligned(start, length):
        return pl.ds(pl.multiple_of(start, ROW_TILE), length)

    fields = (((xa0, xm0), (xb0, xn0)), ((xa1, xm1), (xb1, xn1)))
    cores = (core, 1 - core)
    chips = (chip, 1 - chip)
    mine = [pl.ds(h * piece, piece) for h in range(PIECES)]
    made, started, to_relays, from_relays = {}, [], [], []

    def remote(key, src, dst, target):
        if key not in made:
            i = len(made)
            made[key] = pltpu.make_async_remote_copy(
                src_ref=src, dst_ref=dst, send_sem=send_sem.at[i], recv_sem=recv_sem.at[i],
                device_id=target, device_id_type=MESH_ID)
        return made[key]

    def direct(step, g, h):
        x, rows = fields[step][g][0], mine[h]
        return remote(("direct", step, g, h), x.at[1, rows], x.at[0, rows], {"sec": direct_to})

    def relay(step, g, h):
        x, rows = fields[step][g][0], mine[h]
        return remote(("relay", step, g, h), x.at[0, rows], x.at[2, rows], {"sec": relay_to})

    def to_core(step, g, h, slot):
        (x, y), rows = fields[step][g], mine[h]
        return remote(("core", step, g, h, slot), x.at[slot, rows], y.at[slot, rows], {"ops": mate})

    def to_other(step, h, slot):
        x, y, rows = fields[step][0][0], fields[step][1][0], mine[h]
        return remote(("other", step, h, slot), x.at[slot, rows], y.at[slot, rows], {"ops": across})

    def go(copy):
        copy.start()
        started.append(copy)

    def crossing(step, g, h):
        return step == 0 and g == 0 and h >= STRAIGHT

    def direct_in(step, g, h):
        direct(step, g, h).wait_recv()
        onward = relay(step, g, h)
        to_relays.append(onward)

        @pl.when(has_target)
        def _():
            onward.start()

        go(to_core(step, g, h, 0))
        if crossing(step, g, h):
            go(to_other(step, h, 0))

    def relay_in(step, g, h):
        copies = [to_core(step, g, h, 2)]
        if crossing(step, g, h):
            copies.append(to_other(step, h, 2))
        from_relays.extend(copies)
        arriving = relay(step, g, h)

        @pl.when(has_source)
        def _():
            arriving.wait_recv()
            for copy in copies:
                copy.start()

    def twin_in(step, h):
        part = mine[h]
        twin[h].wait_recv()
        summed = (
            acc_far[part, :]
            + from_mate[step, 0, part, :].astype(jnp.float32)
            + from_twin[part, :].astype(jnp.float32)
        )
        first = (1 - chip) * half + core * share + h * piece
        fields[1][1][0][1, part, :] = masked(summed * scale, first).astype(jnp.bfloat16)
        go(direct(1, 1, h))
        go(to_core(1, 1, h, 1))

    def cross_in(step, h):
        to_other(step, h, 0).wait_recv()
        go(to_core(step, 1, h, 0))
        copy = to_core(step, 1, h, 2)
        from_relays.append(copy)
        arriving = to_other(step, h, 2)

        @pl.when(has_source)
        def _():
            arriving.wait_recv()
            copy.start()

    picks = [1 - (1 - 2 * parity) * charge_ref[0, p] for p in range(pairs)]

    def right_products(step, g, m):
        if m:
            for h in range(PIECES):
                to_core(step, g, h, 0).wait_recv()
                if step:
                    to_core(step, g, h, 1).wait_recv()
            arriving = [to_core(step, g, h, 2) for h in range(PIECES)]

            @pl.when(has_source)
            def _():
                for copy in arriving:
                    copy.wait_recv()

        x = fields[step][g][m]
        for p in range(pairs):
            y_buf[aligned(p * width + chips[g] * half + cores[m] * share, share), :] = (
                lax.dot_general(
                    x[picks[p]], r_buf[p], (((1,), (1,)), ((), ())),
                    preferred_element_type=jnp.float32).astype(jnp.bfloat16))

    def left_products(g, owner):
        return jnp.dot(l_buf[aligned(chips[g] * half + owner * share, share), :], y_buf[...],
                       preferred_element_type=jnp.float32)

    hand, ship, twin = {}, {}, {}

    def left_and_send(step):
        for k in range(2):
            for h in range(PIECES):
                hand[k, h] = remote(
                    ("hand", step, k, h), to_mate.at[step, k, mine[h]],
                    from_mate.at[step, k, mine[h]], {"ops": mate})
        to_mate[step, 0] = left_products(1, 1 - core).astype(jnp.bfloat16)
        for h in range(PIECES):
            go(hand[0, h])
        acc_far[...] = left_products(1, core)
        to_mate[step, 1] = left_products(0, 1 - core).astype(jnp.bfloat16)
        for h in range(PIECES):
            go(hand[1, h])
        for h in range(PIECES):
            part = mine[h]
            hand[0, h].wait_recv()
            to_chip[step, part, :] = (
                acc_far[part, :] + from_mate[step, 0, part, :].astype(jnp.float32)
            ).astype(jnp.bfloat16)
            ship[h] = remote(
                ("ship", step, h), to_chip.at[step, part], from_chip.at[step, part],
                {"ops": across})
            go(ship[h])
        acc_near[...] = left_products(0, core)
        for h in range(PIECES):
            part = mine[h]
            hand[1, h].wait_recv()
            if step + 1 < STEPS:
                to_twin[part, :] = (
                    acc_near[part, :] + from_mate[step, 1, part, :].astype(jnp.float32)
                ).astype(jnp.bfloat16)
                twin[h] = remote(
                    ("twin", step, h), to_twin.at[part], from_twin.at[part], {"ops": across})
                go(twin[h])

    def finish(step, h):
        part = pl.ds(h * piece, piece)
        first = o * share + h * piece
        ship[h].wait_recv()
        summed = (
            acc_near[part, :]
            + from_mate[step, 1, part, :].astype(jnp.float32)
            + from_chip[step, part, :].astype(jnp.float32)
        )
        live = masked(summed, first)
        applied = live * scale
        if step == 0:
            prev_ref[0, part, :] = live
            fields[1][0][0][1, part, :] = applied.astype(jnp.bfloat16)
            go(direct(1, 0, h))
            go(to_core(1, 0, h, 1))
        else:
            start_rows = masked(v_buf[aligned(first, piece), :], first)
            last_ref[0, part, :] = applied - 0.5 * start_rows

    v_copy.wait()
    for load in loads:
        load.start()
    for g in range(2):
        for m in range(2):
            first = chips[g] * half + cores[m] * share
            fields[0][g][m][1] = masked(
                v_buf[aligned(first, share), :], first).astype(jnp.bfloat16)
    pl.semaphore_wait(barrier, 3 + has_target.astype(jnp.int32) + has_source.astype(jnp.int32))
    turns = [(0, h) for h in range(STRAIGHT, PIECES)]
    turns += [(g, h) for g in range(2) for h in range(STRAIGHT)]
    for g, h in turns:
        go(direct(0, g, h))

    @pl.when(jnp.logical_not(has_source))
    def _():
        for field in fields:
            for x in (*field[0], *field[1]):
                x[2] = jnp.zeros(x.shape[1:], x.dtype)

    lag, behind = 3, 3
    events = []
    for k, (g, h) in enumerate(turns):
        events.append((k, direct_in, (0, g, h)))
        events.append((k + lag, relay_in, (0, g, h)))
        if crossing(0, g, h):
            events.append((k + 3 * lag, cross_in, (0, h)))
    for load in loads[:pairs]:
        events.append((PIECES, load.wait, ()))
    events.append((PIECES + lag, right_products, (0, 0, 0)))
    events.append((PIECES + lag, right_products, (0, 0, 1)))
    for _, run, arguments in sorted(events, key=lambda event: event[0]):
        run(*arguments)
    right_products(0, 1, 0)
    right_products(0, 1, 1)
    for load in loads[pairs:]:
        load.wait()
    left_and_send(0)

    events = []
    for h in range(PIECES):
        events.append((h, finish, (0, h)))
        events.append((h + behind, direct_in, (1, 0, h)))
        events.append((h + behind + lag, relay_in, (1, 0, h)))
        events.append((h + PIECES, twin_in, (0, h)))
        events.append((h + PIECES + behind, direct_in, (1, 1, h)))
        events.append((h + PIECES + behind + lag, relay_in, (1, 1, h)))
    events.append((2 * PIECES + behind - 1, right_products, (1, 0, 0)))
    events.append((2 * PIECES + behind, right_products, (1, 0, 1)))
    for _, run, arguments in sorted(events, key=lambda event: event[0]):
        run(*arguments)
    right_products(1, 1, 0)
    right_products(1, 1, 1)
    left_and_send(1)
    for h in range(PIECES):
        finish(1, h)

    for copy in started:
        copy.wait_send()

    @pl.when(has_target)
    def _():
        for copy in to_relays:
            copy.wait_send()

    @pl.when(has_source)
    def _():
        for copy in from_relays:
            copy.wait_send()


def by_kernel(wavefunction, left_ops, right_ops, charge_step, sector_sizes):
    ops_count, sectors = lax.axis_size("ops"), lax.axis_size("sec")
    pairs, width = left_ops.shape[1], left_ops.shape[2]
    share = width // ops_count
    stay = pl.BlockSpec(memory_space=pltpu.HBM)
    vmem = pl.BlockSpec(memory_space=pltpu.VMEM)
    bf16, f32 = jnp.bfloat16, jnp.float32
    field = pltpu.VMEM((3, share, width), bf16)
    copies = STEPS * (2 * PIECES * 5 + 6 * PIECES)
    out = jax.ShapeDtypeStruct((1, share, width), f32)
    raw = pl.pallas_call(
        functools.partial(kernel, ops_count, sectors),
        out_shape=(out, out),
        in_specs=[stay] * 5,
        out_specs=(vmem, vmem),
        scratch_shapes=[
            pltpu.SMEM((1, pairs), jnp.int32),
            pltpu.SMEM((sectors,), jnp.int32),
            pltpu.VMEM((width, width), f32),
            pltpu.VMEM((width, pairs * width), bf16),
            pltpu.VMEM((pairs, width, width), bf16),
            *[field] * 8,
            pltpu.VMEM((pairs * width, width), bf16),
            pltpu.VMEM((share, width), f32),
            pltpu.VMEM((share, width), f32),
            pltpu.VMEM((STEPS, 2, share, width), bf16),
            pltpu.VMEM((STEPS, 2, share, width), bf16),
            pltpu.VMEM((STEPS, share, width), bf16),
            pltpu.VMEM((STEPS, share, width), bf16),
            pltpu.VMEM((share, width), bf16),
            pltpu.VMEM((share, width), bf16),
            pltpu.SemaphoreType.DMA((3 + 2 * pairs,)),
            pltpu.SemaphoreType.DMA((copies,)),
            pltpu.SemaphoreType.DMA((copies,)),
        ],
        compiler_params=pltpu.CompilerParams(
            collective_id=0, has_side_effects=True, vmem_limit_bytes=67_043_328),
    )(wavefunction, left_ops, right_ops, charge_step, sector_sizes)
    return raw[0] * (1.0 / math.sqrt(pairs * ops_count)), raw[1] * 2.0


def on_device(wavefunction, left_ops, right_ops, charge_step, sector_sizes):
    ops_count, sectors = lax.axis_size("ops"), lax.axis_size("sec")
    share = wavefunction.shape[1] // ops_count
    paired = ops_count == 2 * CORES and sectors % 2 == 0
    tiled = share % (PIECES * ROW_TILE) == 0
    body = by_kernel if paired and tiled else by_collectives
    return body(wavefunction, left_ops, right_ops, charge_step, sector_sizes)


def solution(mesh):
    in_specs = (
        P("sec", None, None),
        P("sec", "ops", None, None),
        P("sec", "ops", None, None),
        P("sec", "ops"),
        P(),
    )
    out_specs = (P("sec", "ops", None), P("sec", "ops", None))
    return jax.shard_map(
        on_device, mesh=mesh, in_specs=in_specs, out_specs=out_specs, check_vma=False
    )
```

```python
import functools
import math

import jax
import jax.numpy as jnp
from jax import lax
from jax.experimental import pallas as pl
from jax.experimental.pallas import tpu as pltpu
from jax.sharding import PartitionSpec as P

STEPS = 2
CORES = 2
PIECES = 5
STRAIGHT = 3
LAG = 4
BEHIND = 5
ROW_TILE = 16
MESH_ID = pl.DeviceIdType.MESH


def padded(shard, sides, width):
    for axis, dim in sides:
        peers, length = (lax.axis_size(axis), shard.shape[dim])
        up = [(i, (i + 1) % peers) for i in range(peers - 1)]
        down = [(j, i) for i, j in up]
        last = lax.slice_in_dim(shard, length - width, length, axis=dim)
        initial = lax.slice_in_dim(shard, 0, width, axis=dim)
        before = lax.ppermute(last, axis, up)
        after = lax.ppermute(initial, axis, down)
        shard = jnp.concatenate([before, shard, after], axis=dim)
    return shard


def by_collectives(wavefunction, left_ops, right_ops, charge_step, sector_sizes):
    ops_count = lax.axis_size("ops")
    width_all = wavefunction.shape[1]
    share_rows = width_all // ops_count
    first_row = lax.axis_index("ops") * share_rows
    own_size = lax.dynamic_index_in_dim(sector_sizes, lax.axis_index("sec"), 0, keepdims=False)
    positions = jnp.arange(width_all, dtype=jnp.int32)
    live_cols = (positions < own_size).astype(jnp.float32)
    row_live = lax.dynamic_slice_in_dim(live_cols, first_row, share_rows, 0)
    full_mask = live_cols[:, None] * live_cols[None, :]
    row_mask = row_live[:, None] * live_cols[None, :]
    norm_scale = 1.0 / math.sqrt(left_ops.shape[1] * ops_count)
    onehot = (charge_step[0][:, None] + 1 == jnp.arange(3, dtype=jnp.int32)[None, :]).astype(
        jnp.bfloat16
    )
    start_field = wavefunction[0] * full_mask
    start_rows = lax.dynamic_slice_in_dim(start_field, first_row, share_rows, 0)
    previous = start_rows
    current = start_rows
    source_full = start_field.astype(jnp.bfloat16)
    for iteration in range(STEPS):
        nearby = padded(source_full[None], (("sec", 0),), 1)
        inputs = jnp.einsum(
            "pc,cab->pab", onehot, nearby, preferred_element_type=jnp.float32
        ).astype(jnp.bfloat16)
        left_half = jnp.einsum(
            "pab,pbc->pac", left_ops[0], inputs, preferred_element_type=jnp.float32
        ).astype(jnp.bfloat16)
        summed = lax.psum_scatter(
            jnp.einsum("pac,pdc->ad", left_half, right_ops[0], preferred_element_type=jnp.float32),
            "ops",
            scatter_dimension=0,
            tiled=True,
        )
        applied = summed * norm_scale * row_mask
        updated = applied if iteration == 0 else 2.0 * applied - previous
        previous = start_rows if iteration == 0 else current
        current = updated
        if iteration + 1 < STEPS:
            source_full = lax.all_gather(updated.astype(jnp.bfloat16), "ops", axis=0, tiled=True)
    return (previous[None], current[None])


def kernel(
    ops_count, sectors,
    v_hbm, l_hbm, r_hbm, charge_hbm, size_hbm, prev_ref, last_ref,
    charge_ref, size_ref, v_buf, l_buf, r_buf, xa0, xm0, xb0, xn0, xa1, xm1, xb1, xn1, y_buf,
    acc_far, acc_near, to_mate, from_mate, to_chip, from_chip, to_twin, from_twin,
    local_sem, send_sem, recv_sem,
):
    pairs, width = l_hbm.shape[1], l_hbm.shape[2]
    share = width // ops_count
    half = CORES * share
    piece = share // PIECES
    scale = 1.0 / math.sqrt(pairs * ops_count)

    o = lax.axis_index("ops")
    t = lax.axis_index("sec")
    core = lax.rem(o, CORES)
    chip = o // CORES
    mate = o + 1 - 2 * core
    across = lax.rem(o + CORES, ops_count)
    parity = lax.rem(t, 2)
    direct_to = t + 1 - 2 * parity
    relay_to = t + 2 - 4 * parity
    relay_from = t - 2 + 4 * parity
    has_target = jnp.logical_and(relay_to >= 0, relay_to < sectors)
    has_source = jnp.logical_and(relay_from >= 0, relay_from < sectors)

    v_copy = pltpu.make_async_copy(v_hbm.at[0], v_buf, local_sem.at[0])
    smalls = [pltpu.make_async_copy(size_hbm, size_ref, local_sem.at[1 + 2 * pairs]),
              pltpu.make_async_copy(charge_hbm, charge_ref, local_sem.at[2 + 2 * pairs])]
    v_copy.start()
    for small in smalls:
        small.start()
    loads = []
    for p in range(pairs):
        loads.append(pltpu.make_async_copy(r_hbm.at[0, p], r_buf.at[p], local_sem.at[1 + p]))
    for p in range(pairs):
        loads.append(pltpu.make_async_copy(
            l_hbm.at[0, p], l_buf.at[:, pl.ds(p * width, width)], local_sem.at[1 + pairs + p]))

    barrier = pltpu.get_barrier_semaphore()
    pl.semaphore_signal(barrier, inc=1, device_id={"ops": mate}, device_id_type=MESH_ID)
    pl.semaphore_signal(barrier, inc=1, device_id={"ops": across}, device_id_type=MESH_ID)
    pl.semaphore_signal(barrier, inc=1, device_id={"sec": direct_to}, device_id_type=MESH_ID)

    @pl.when(has_target)
    def _():
        pl.semaphore_signal(barrier, inc=1, device_id={"sec": relay_to}, device_id_type=MESH_ID)

    @pl.when(has_source)
    def _():
        pl.semaphore_signal(barrier, inc=1, device_id={"sec": relay_from}, device_id_type=MESH_ID)

    for small in smalls:
        small.wait()
    size = size_ref[t]
    cols_live = lax.broadcasted_iota(jnp.int32, (1, width), 1) < size

    def masked(value, first):
        rows = first + lax.broadcasted_iota(jnp.int32, (value.shape[0], 1), 0)
        return jnp.where(jnp.logical_and(rows < size, cols_live), value, 0.0)

    def aligned(start, length):
        return pl.ds(pl.multiple_of(start, ROW_TILE), length)

    fields = (((xa0, xm0), (xb0, xn0)), ((xa1, xm1), (xb1, xn1)))
    cores = (core, 1 - core)
    chips = (chip, 1 - chip)
    mine = [pl.ds(h * piece, piece) for h in range(PIECES)]
    made, started, to_relays, from_relays = {}, [], [], []

    def remote(key, src, dst, target):
        if key not in made:
            i = len(made)
            made[key] = pltpu.make_async_remote_copy(
                src_ref=src, dst_ref=dst, send_sem=send_sem.at[i], recv_sem=recv_sem.at[i],
                device_id=target, device_id_type=MESH_ID)
        return made[key]

    def direct(step, g, h):
        x, rows = fields[step][g][0], mine[h]
        return remote(("direct", step, g, h), x.at[1, rows], x.at[0, rows], {"sec": direct_to})

    def relay(step, g, h):
        x, rows = fields[step][g][0], mine[h]
        return remote(("relay", step, g, h), x.at[0, rows], x.at[2, rows], {"sec": relay_to})

    def to_core(step, g, h, slot):
        (x, y), rows = fields[step][g], mine[h]
        return remote(("core", step, g, h, slot), x.at[slot, rows], y.at[slot, rows], {"ops": mate})

    def to_other(step, h, slot):
        x, y, rows = fields[step][0][0], fields[step][1][0], mine[h]
        return remote(("other", step, h, slot), x.at[slot, rows], y.at[slot, rows], {"ops": across})

    def go(copy):
        copy.start()
        started.append(copy)

    def crossing(step, g, h):
        return step == 0 and g == 0 and h >= STRAIGHT

    def direct_in(step, g, h):
        direct(step, g, h).wait_recv()
        onward = relay(step, g, h)
        to_relays.append(onward)

        @pl.when(has_target)
        def _():
            onward.start()

        go(to_core(step, g, h, 0))
        if crossing(step, g, h):
            go(to_other(step, h, 0))

    def relay_in(step, g, h):
        copies = [to_core(step, g, h, 2)]
        if crossing(step, g, h):
            copies.append(to_other(step, h, 2))
        from_relays.extend(copies)
        arriving = relay(step, g, h)

        @pl.when(has_source)
        def _():
            arriving.wait_recv()
            for copy in copies:
                copy.start()

    def twin_in(step, h):
        part = mine[h]
        twin[h].wait_recv()
        summed = (
            acc_far[part, :]
            + from_mate[step, 0, part, :].astype(jnp.float32)
            + from_twin[part, :].astype(jnp.float32)
        )
        first = (1 - chip) * half + core * share + h * piece
        fields[1][1][0][1, part, :] = masked(summed * scale, first).astype(jnp.bfloat16)
        go(direct(1, 1, h))
        go(to_core(1, 1, h, 1))

    def cross_in(step, h):
        to_other(step, h, 0).wait_recv()
        go(to_core(step, 1, h, 0))
        copy = to_core(step, 1, h, 2)
        from_relays.append(copy)
        arriving = to_other(step, h, 2)

        @pl.when(has_source)
        def _():
            arriving.wait_recv()
            copy.start()

    picks = [1 - (1 - 2 * parity) * charge_ref[0, p] for p in range(pairs)]

    def right_products(step, g, m):
        if m:
            for h in range(PIECES):
                to_core(step, g, h, 0).wait_recv()
                if step:
                    to_core(step, g, h, 1).wait_recv()
            arriving = [to_core(step, g, h, 2) for h in range(PIECES)]

            @pl.when(has_source)
            def _():
                for copy in arriving:
                    copy.wait_recv()

        x = fields[step][g][m]
        for p in range(pairs):
            y_buf[aligned(p * width + chips[g] * half + cores[m] * share, share), :] = (
                lax.dot_general(
                    x[picks[p]], r_buf[p], (((1,), (1,)), ((), ())),
                    preferred_element_type=jnp.float32).astype(jnp.bfloat16))

    def left_products(g, owner):
        return jnp.dot(l_buf[aligned(chips[g] * half + owner * share, share), :], y_buf[...],
                       preferred_element_type=jnp.float32)

    hand, ship, twin = {}, {}, {}

    def left_and_send(step):
        for k in range(2):
            for h in range(PIECES):
                hand[k, h] = remote(
                    ("hand", step, k, h), to_mate.at[step, k, mine[h]],
                    from_mate.at[step, k, mine[h]], {"ops": mate})
        to_mate[step, 0] = left_products(1, 1 - core).astype(jnp.bfloat16)
        for h in range(PIECES):
            go(hand[0, h])
        acc_far[...] = left_products(1, core)
        to_mate[step, 1] = left_products(0, 1 - core).astype(jnp.bfloat16)
        for h in range(PIECES):
            go(hand[1, h])
        for h in range(PIECES):
            part = mine[h]
            hand[0, h].wait_recv()
            to_chip[step, part, :] = (
                acc_far[part, :] + from_mate[step, 0, part, :].astype(jnp.float32)
            ).astype(jnp.bfloat16)
            ship[h] = remote(
                ("ship", step, h), to_chip.at[step, part], from_chip.at[step, part],
                {"ops": across})
            go(ship[h])
        acc_near[...] = left_products(0, core)
        for h in range(PIECES):
            part = mine[h]
            hand[1, h].wait_recv()
            if step + 1 < STEPS:
                to_twin[part, :] = (
                    acc_near[part, :] + from_mate[step, 1, part, :].astype(jnp.float32)
                ).astype(jnp.bfloat16)
                twin[h] = remote(
                    ("twin", step, h), to_twin.at[part], from_twin.at[part], {"ops": across})
                go(twin[h])

    def finish(step, h):
        part = pl.ds(h * piece, piece)
        first = o * share + h * piece
        ship[h].wait_recv()
        summed = (
            acc_near[part, :]
            + from_mate[step, 1, part, :].astype(jnp.float32)
            + from_chip[step, part, :].astype(jnp.float32)
        )
        live = masked(summed, first)
        applied = live * scale
        if step == 0:
            prev_ref[0, part, :] = live
            fields[1][0][0][1, part, :] = applied.astype(jnp.bfloat16)
            go(direct(1, 0, h))
            go(to_core(1, 0, h, 1))
        else:
            start_rows = masked(v_buf[aligned(first, piece), :], first)
            last_ref[0, part, :] = applied - 0.5 * start_rows

    v_copy.wait()
    for load in loads:
        load.start()
    for g in range(2):
        for m in range(2):
            first = chips[g] * half + cores[m] * share
            fields[0][g][m][1] = masked(
                v_buf[aligned(first, share), :], first).astype(jnp.bfloat16)
    pl.semaphore_wait(barrier, 3 + has_target.astype(jnp.int32) + has_source.astype(jnp.int32))
    turns = [(0, h) for h in range(STRAIGHT, PIECES)]
    turns += [(g, h) for g in range(2) for h in range(STRAIGHT)]
    for g, h in turns:
        go(direct(0, g, h))

    @pl.when(jnp.logical_not(has_source))
    def _():
        for field in fields:
            for x in (*field[0], *field[1]):
                x[2] = jnp.zeros(x.shape[1:], x.dtype)

    lag, behind = LAG, BEHIND
    events = []
    for k, (g, h) in enumerate(turns):
        events.append((k, direct_in, (0, g, h)))
        events.append((k + lag, relay_in, (0, g, h)))
        if crossing(0, g, h):
            events.append((k + 3 * lag, cross_in, (0, h)))
    for load in loads[:pairs]:
        events.append((PIECES, load.wait, ()))
    events.append((PIECES + lag, right_products, (0, 0, 0)))
    events.append((PIECES + lag, right_products, (0, 0, 1)))
    for _, run, arguments in sorted(events, key=lambda event: event[0]):
        run(*arguments)
    right_products(0, 1, 0)
    right_products(0, 1, 1)
    for load in loads[pairs:]:
        load.wait()
    left_and_send(0)

    events = []
    for h in range(PIECES):
        events.append((h, finish, (0, h)))
        events.append((h + behind, direct_in, (1, 0, h)))
        events.append((h + behind + lag, relay_in, (1, 0, h)))
        events.append((h + PIECES, twin_in, (0, h)))
        events.append((h + PIECES + behind, direct_in, (1, 1, h)))
        events.append((h + PIECES + behind + lag, relay_in, (1, 1, h)))
    events.append((2 * PIECES + behind - 1, right_products, (1, 0, 0)))
    events.append((2 * PIECES + behind, right_products, (1, 0, 1)))
    for _, run, arguments in sorted(events, key=lambda event: event[0]):
        run(*arguments)
    right_products(1, 1, 0)
    right_products(1, 1, 1)
    left_and_send(1)
    for h in range(PIECES):
        finish(1, h)

    for copy in started:
        copy.wait_send()

    @pl.when(has_target)
    def _():
        for copy in to_relays:
            copy.wait_send()

    @pl.when(has_source)
    def _():
        for copy in from_relays:
            copy.wait_send()


def by_kernel(wavefunction, left_ops, right_ops, charge_step, sector_sizes):
    ops_count, sectors = lax.axis_size("ops"), lax.axis_size("sec")
    pairs, width = left_ops.shape[1], left_ops.shape[2]
    share = width // ops_count
    stay = pl.BlockSpec(memory_space=pltpu.HBM)
    vmem = pl.BlockSpec(memory_space=pltpu.VMEM)
    bf16, f32 = jnp.bfloat16, jnp.float32
    field = pltpu.VMEM((3, share, width), bf16)
    copies = STEPS * (2 * PIECES * 5 + 6 * PIECES)
    out = jax.ShapeDtypeStruct((1, share, width), f32)
    raw = pl.pallas_call(
        functools.partial(kernel, ops_count, sectors),
        out_shape=(out, out),
        in_specs=[stay] * 5,
        out_specs=(vmem, vmem),
        scratch_shapes=[
            pltpu.SMEM((1, pairs), jnp.int32),
            pltpu.SMEM((sectors,), jnp.int32),
            pltpu.VMEM((width, width), f32),
            pltpu.VMEM((width, pairs * width), bf16),
            pltpu.VMEM((pairs, width, width), bf16),
            *[field] * 8,
            pltpu.VMEM((pairs * width, width), bf16),
            pltpu.VMEM((share, width), f32),
            pltpu.VMEM((share, width), f32),
            pltpu.VMEM((STEPS, 2, share, width), bf16),
            pltpu.VMEM((STEPS, 2, share, width), bf16),
            pltpu.VMEM((STEPS, share, width), bf16),
            pltpu.VMEM((STEPS, share, width), bf16),
            pltpu.VMEM((share, width), bf16),
            pltpu.VMEM((share, width), bf16),
            pltpu.SemaphoreType.DMA((3 + 2 * pairs,)),
            pltpu.SemaphoreType.DMA((copies,)),
            pltpu.SemaphoreType.DMA((copies,)),
        ],
        compiler_params=pltpu.CompilerParams(
            collective_id=0, has_side_effects=True, vmem_limit_bytes=67_043_328),
    )(wavefunction, left_ops, right_ops, charge_step, sector_sizes)
    return raw[0] * (1.0 / math.sqrt(pairs * ops_count)), raw[1] * 2.0


def on_device(wavefunction, left_ops, right_ops, charge_step, sector_sizes):
    ops_count, sectors = lax.axis_size("ops"), lax.axis_size("sec")
    share = wavefunction.shape[1] // ops_count
    paired = ops_count == 2 * CORES and sectors % 2 == 0
    tiled = share % (PIECES * ROW_TILE) == 0
    body = by_kernel if paired and tiled else by_collectives
    return body(wavefunction, left_ops, right_ops, charge_step, sector_sizes)


def solution(mesh):
    in_specs = (
        P("sec", None, None),
        P("sec", "ops", None, None),
        P("sec", "ops", None, None),
        P("sec", "ops"),
        P(),
    )
    out_specs = (P("sec", "ops", None), P("sec", "ops", None))
    return jax.shard_map(
        on_device, mesh=mesh, in_specs=in_specs, out_specs=out_specs, check_vma=False
    )
```
